1024 devices in a mesh: ctx: 32 (over z, core), head: 32 (over y, x).
Axes of the slice: x: 4, y: 8, z: 16, core: 2. Of those that a mesh axis runs over, the one named last changes fastest.
Arguments:
- queries: bfloat16 [98304, 4096], P(('ctx', 'head')), may hold values from -6 to 6
- keys: bfloat16 [98304, 4096], P(('ctx', 'head')), may hold values from -6 to 6
- values: bfloat16 [98304, 4096], P(('ctx', 'head')), may hold values from -6 to 6
- log_decay: bfloat16 [98304, 32], P(('ctx', 'head')), as said below
- gain: float32 [4096], P('head'), may hold values from 0.1 to 1.9
- doc_starts: int32 [9], replicated, may hold values from 0 to 98304, as said below
Outputs:
- attended: bfloat16 [98304, 4096], P(('ctx', 'head'))
The draws below stay inside these ranges and needn't reach their ends.
Inputs may be any that keep to these rules, and one draw needn't show every extreme that they name: doc_starts begins with 0, ends with 98304 and rises strictly; the first document holds at least 61440 tokens. `log_decay`: entries are at most 0.
All inputs are finite; a program needn't handle non-finite values.
Results may differ from the reference program's by a relative error of at most 0.0049.
Values may be sent and summed in bfloat16 or wider, within the bound.
No kernel may reach another device: no remote copies, remote signals or barrier semaphores. Data moves between devices by JAX's collectives and lax.ppermute only.
A program may use at most 32 MiB of HBM per device.

```python
import math
import jax
import jax.numpy as jnp
from jax import lax

E = 128
H = 32
SEQUENCE_TOKENS = 98304
BLOCK = 512
NDOC = 8


def draw_log_decay(key, part):
    keys = jax.random.split(key, 6)
    fast_share = 0.5
    fast = jax.random.uniform(keys[0], (H,)) < fast_share
    fast_rate = 1.0 / jax.random.uniform(keys[1], (H,), minval=30.0, maxval=50.0)
    slow_factor = jnp.exp(jax.random.uniform(keys[2], (H,), minval=math.log(0.5), maxval=math.log(16.0)))
    slow_rate = math.log(2.0) / SEQUENCE_TOKENS * slow_factor
    decay_speed = jnp.where(fast, fast_rate, slow_rate)
    decay_multiplier = jnp.exp(jax.random.uniform(keys[3], (SEQUENCE_TOKENS, H), minval=math.log(0.5), maxval=math.log(2.0)))
    window_position = jax.random.randint(keys[4], (2,), 0, SEQUENCE_TOKENS)
    window_retained = jax.random.uniform(keys[5], (2,), minval=0.5, maxval=0.8)
    token_positions = jnp.arange(SEQUENCE_TOKENS, dtype=jnp.int32)
    decay_window = jnp.sum(jnp.where(token_positions[:, None] == window_position[None, :], jnp.log(window_retained)[None, :], 0.0), axis=1)
    return (-decay_speed[None, :] * decay_multiplier + decay_window[:, None]).astype(jnp.bfloat16)


def draw_doc_starts(key, part):
    lower = 5 * SEQUENCE_TOKENS // 8
    slot = (SEQUENCE_TOKENS - lower) // (NDOC - 1)
    offsets = jax.random.randint(key, (NDOC - 1,), 0, slot)
    inner = lower + jnp.arange(NDOC - 1, dtype=jnp.int32) * slot + offsets
    head_part = jnp.zeros((1,), jnp.int32)
    tail_part = jnp.full((1,), SEQUENCE_TOKENS, jnp.int32)
    return jnp.concatenate([head_part, inner.astype(jnp.int32), tail_part]).astype(jnp.int32)


def levels(own_key, extent, pieces, smallest, largest):
    loudness, own = 1.0, jax.random.fold_in(own_key, 6)
    for position, shards_of in pieces:
        draws = jnp.exp(jax.random.uniform(jax.random.fold_in(own, position), (shards_of,), jnp.float32, smallest / len(pieces), largest / len(pieces)))
        loudness = loudness * jnp.repeat(draws, extent[position] // shards_of).reshape([-1 if axis == position else 1 for axis in range(len(extent))])
    return loudness


def normal_values(rng, extent, width, limit, pieces=(), kind=jnp.bfloat16):
    drawn = width * jax.random.normal(rng, extent, jnp.float32)
    if pieces:
        drawn = drawn * levels(rng, extent, pieces, -0.22, 0.18)
    return jnp.clip(drawn, -limit, limit).astype(kind)


def setup_inputs(seed: int = 0) -> dict:
    seeds = jax.random.split(jax.random.key(seed), 7)
    return {
        "queries": normal_values(seeds[0], (SEQUENCE_TOKENS, H * E), 1.0, 6.0, ((0, 1024),)),
        "keys": normal_values(seeds[1], (SEQUENCE_TOKENS, H * E), 1.0, 6.0, ((0, 1024),)),
        "values": normal_values(seeds[2], (SEQUENCE_TOKENS, H * E), 1.0, 6.0, ((0, 1024),)),
        "log_decay": draw_log_decay(jax.random.fold_in(seeds[6], 71), 0),
        "gain": jnp.clip(1.0 + 0.18 * jax.random.normal(seeds[4], (H * E,), jnp.float32), 0.1, 1.9),
        "doc_starts": draw_doc_starts(jax.random.fold_in(seeds[6], 71), 0),
    }


def reference(queries, keys, values, log_decay, gain, doc_starts):
    nblk = SEQUENCE_TOKENS // BLOCK
    token_positions = jnp.arange(SEQUENCE_TOKENS, dtype=jnp.int32)
    doc_id = lax.optimization_barrier(jnp.sum((token_positions[:, None] >= doc_starts[None, 1:NDOC]).astype(jnp.int32), axis=1))
    is_start = jnp.any(token_positions[:, None] == doc_starts[None, 0:NDOC], axis=1)
    qb = queries.reshape(nblk, BLOCK, H, E)
    kb = keys.reshape(nblk, BLOCK, H, E)
    vb = values.reshape(nblk, BLOCK, H, E)
    gb = log_decay.reshape(nblk, BLOCK, H)
    docb = doc_id.reshape(nblk, BLOCK)
    startb = is_start.reshape(nblk, BLOCK)
    gain_heads = gain.reshape(H, E)
    rows = jnp.arange(BLOCK, dtype=jnp.int32)

    def step(state, item):
        qx, kx, vx, gx, dx, sx = item
        cum = jnp.cumsum(gx.astype(jnp.float32), axis=0)
        opened = jnp.cumsum(sx.astype(jnp.int32)) == 0
        mask = (rows[None, :] <= rows[:, None]) & (dx[:, None] == dx[None, :])
        cum_t = cum.T
        diff = cum_t[:, :, None] - cum_t[:, None, :]
        decay = jnp.where(mask[None], jnp.exp(jnp.where(mask[None], diff, 0.0)), 0.0)
        scores = jnp.einsum('thd,jhd->htj', qx.astype(jnp.float32), kx.astype(jnp.float32))
        weights = (scores * decay).astype(jnp.bfloat16)
        intra = jnp.einsum('htj,jhe->the', weights.astype(jnp.float32), vx.astype(jnp.float32))
        reach = jnp.exp(cum) * opened[:, None].astype(jnp.float32)
        scaled_q = qx.astype(jnp.float32) * reach[:, :, None]
        inter = jnp.einsum('the,hef->thf', scaled_q, state, precision=lax.Precision.HIGHEST)
        attn = intra + inter
        meansq = lax.optimization_barrier(jnp.mean(attn * attn, axis=-1, keepdims=True))
        normed = attn * lax.rsqrt(meansq + 1e-05) * gain_heads[None]
        last = cum[-1]
        tail = jnp.exp(last[None, :] - cum) * (dx == dx[-1])[:, None].astype(jnp.float32)
        scaled_keys = (kx.astype(jnp.float32) * tail[:, :, None]).astype(jnp.bfloat16)
        summary = jnp.einsum('jhe,jhf->hef', scaled_keys.astype(jnp.float32), vx.astype(jnp.float32))
        keep = jnp.exp(last) * opened[-1].astype(jnp.float32)
        state = keep[:, None, None] * state + summary
        return (state, normed.astype(jnp.bfloat16).reshape(BLOCK, H * E))
    init = jnp.zeros((H, E, E), jnp.float32)
    final_state, outs = lax.scan(step, init, (qb, kb, vb, gb, docb, startb))
    return outs.reshape(SEQUENCE_TOKENS, H * E)
```

```python
import functools

import jax
import jax.numpy as jnp
from jax import lax
from jax.experimental import pallas as pl
from jax.experimental.pallas import tpu as pltpu
from jax.sharding import Mesh, PartitionSpec as P

E = 128
HALF = E // 2
PAD = 8
AXES = ("z", "core", "y", "x")
PLANE = ("core", "y", "x")
F32, BF16 = jnp.float32, jnp.bfloat16
VMEM = pl.BlockSpec(memory_space=pltpu.VMEM)
ANY = pl.BlockSpec(memory_space=pl.ANY)
SMEM = pl.BlockSpec(memory_space=pltpu.SMEM)


def started(position, starts_ref):
    count = jnp.zeros_like(position)
    for i in range(starts_ref.shape[0] - 1):
        count = count + (position >= starts_ref[i]).astype(jnp.int32)
    return count


def cumulative(decay_ref):
    tokens = decay_ref.shape[0]
    i = lax.broadcasted_iota(jnp.int32, (tokens, tokens), 0)
    j = lax.broadcasted_iota(jnp.int32, (tokens, tokens), 1)
    lower = (i >= j).astype(BF16)
    return jnp.dot(lower, decay_ref[...], preferred_element_type=F32)


def three_parts(value):
    high = value.astype(BF16).astype(F32)
    middle = (value - high).astype(BF16).astype(F32)
    return high, middle, (value - high - middle).astype(BF16).astype(F32)


def column(h):
    return slice(h * E, (h + 1) * E)


def summarize(first_ref, starts_ref, k_ref, v_ref, decay_ref, gain_ref, out_ref):
    tokens, heads = decay_ref.shape
    first = first_ref[0]
    position = first + lax.broadcasted_iota(jnp.int32, (tokens, 1), 0)
    at_end = started(first + tokens - 1, starts_ref)
    cum = cumulative(decay_ref)
    last = cum[tokens - 1 :, :]
    tail = jnp.where(started(position, starts_ref) == at_end, jnp.exp(last - cum), 0.0)
    open_all = at_end == started(first - 1, starts_ref)
    keep = three_parts(jnp.where(open_all, jnp.exp(last), 0.0))
    gains = three_parts(gain_ref[...])
    row = lax.broadcasted_iota(jnp.int32, (PAD, E), 0)
    base = jnp.zeros((PAD, E), F32)
    for i in range(3):
        base = jnp.where(row == 3 + i, jnp.broadcast_to(gains[i], (PAD, E)), base)
    for h in range(heads):
        scaled = (k_ref[:, column(h)].astype(F32) * tail[:, h : h + 1]).astype(BF16)
        state = lax.dot_general(
            scaled, v_ref[:, column(h)], (((0,), (0,)), ((), ())), preferred_element_type=F32
        ).astype(BF16)
        extra = base
        for i in range(3):
            extra = jnp.where(row == i, jnp.broadcast_to(keep[i][:, h : h + 1], (PAD, E)), extra)
        for c in range(2):
            out_ref[c * heads + h, 0:HALF, :] = state[c * HALF : (c + 1) * HALF]
            out_ref[c * heads + h, HALF : HALF + PAD, :] = extra.astype(BF16)


def within(first_ref, starts_ref, q_ref, k_ref, v_ref, decay_ref, out_ref, done_ref, *, heads):
    done_ref[...] = jnp.zeros_like(done_ref)
    tokens = decay_ref.shape[0]
    first = first_ref[0]
    i = lax.broadcasted_iota(jnp.int32, (tokens, tokens), 0)
    j = lax.broadcasted_iota(jnp.int32, (tokens, tokens), 1)
    mask = (i >= j) & (started(first + i, starts_ref) == started(first + j, starts_ref))
    cum = cumulative(decay_ref)
    across = cum.T
    for n, h in enumerate(heads):
        scores = lax.dot_general(
            q_ref[:, column(h)], k_ref[:, column(h)], (((1,), (1,)), ((), ())), preferred_element_type=F32
        )
        decay = jnp.exp(jnp.where(mask, cum[:, h : h + 1] - across[h : h + 1, :], -1e30))
        weights = (scores * decay).astype(BF16)
        out_ref[:, column(n)] = jnp.dot(weights, v_ref[:, column(h)], preferred_element_type=F32)


def kept(ref, n):
    parts = ref[n, HALF : HALF + PAD, :].astype(F32)
    return parts[0:1] + parts[1:2] + parts[2:3]


def plane_total(got_ref, _, out_ref, gain_ref):
    sources, heads = got_ref.shape[0], gain_ref.shape[0]

    def one(n, carry):
        state, keep = carry
        mine = kept(got_ref, n)
        return mine * state + got_ref[n, 0:HALF, :].astype(F32), mine * keep

    state, keep = lax.fori_loop(
        0, sources, one, (jnp.zeros((HALF, E), F32), jnp.ones((1, E), F32)), unroll=8
    )
    row = lax.broadcasted_iota(jnp.int32, (PAD, E), 0)
    extra = jnp.zeros((PAD, E), F32)
    for i, part in enumerate(three_parts(keep)):
        extra = jnp.where(row == i, jnp.broadcast_to(part, (PAD, E)), extra)
    state, extra = state.astype(BF16), extra.astype(BF16)
    for z in range(out_ref.shape[0]):
        out_ref[z, 0:HALF, :] = state
        out_ref[z, HALF : HALF + PAD, :] = extra
    for h in range(heads):
        parts = got_ref[h, HALF : HALF + PAD, :].astype(F32)
        gain_ref[h : h + 1, :] = parts[3:4] + parts[4:5] + parts[5:6]


def entering(plane_ref, planes_ref, got_ref, _, out_ref):
    def earlier(n, state):
        return kept(planes_ref, n) * state + planes_ref[n, 0:HALF, :].astype(F32)

    def one(n, state):
        out_ref[n] = state.astype(BF16)
        return kept(got_ref, n) * state + got_ref[n, 0:HALF, :].astype(F32)

    state = lax.fori_loop(0, plane_ref[0], earlier, jnp.zeros((HALF, E), F32))
    lax.fori_loop(0, got_ref.shape[0], one, state, unroll=8)


def finish(first_ref, starts_ref, q_ref, decay_ref, *refs):
    *within_refs, enter_ref, gain_ref, out_ref = refs
    tokens, heads = decay_ref.shape
    first = first_ref[0]
    position = first + lax.broadcasted_iota(jnp.int32, (tokens, 1), 0)
    opened = started(position, starts_ref) == started(first - 1, starts_ref)
    reach = jnp.where(opened, jnp.exp(cumulative(decay_ref)), 0.0)
    places = [(ref, n) for ref in within_refs for n in range(ref.shape[1] // E)]
    for h in range(heads):
        ref, n = places[h]
        state = jnp.concatenate([enter_ref[h], enter_ref[heads + h]], axis=0)
        inter = jnp.dot(q_ref[:, column(h)], state, preferred_element_type=F32)
        attn = ref[:, column(n)] + inter * reach[:, h : h + 1]
        meansq = jnp.mean(attn * attn, axis=-1, keepdims=True)
        normed = attn * lax.rsqrt(meansq + 1e-05) * gain_ref[h : h + 1, :]
        out_ref[:, column(h)] = normed.astype(BF16)


def call(kernel, out, specs, name, flops, nbytes):
    return pl.pallas_call(
        kernel,
        out_shape=out,
        in_specs=specs,
        out_specs=jax.tree.map(lambda _: VMEM, out),
        name=name,
        cost_estimate=pl.CostEstimate(flops=flops, bytes_accessed=nbytes, transcendentals=0),
    )


def shared(heads):
    cuts = (0, heads // 2, heads // 2 + heads // 4, heads)
    return [tuple(range(a, b)) for a, b in zip(cuts, cuts[1:])]


def per_device(queries, keys, values, log_decay, gain, doc_starts):
    tokens, heads = log_decay.shape
    planes = lax.axis_size("z")
    sources = 2 * heads
    first = (lax.axis_index(AXES) * tokens).astype(jnp.int32).reshape(1)
    plane = lax.axis_index("z").astype(jnp.int32).reshape(1)
    shape = jax.ShapeDtypeStruct
    tri = 2 * tokens * tokens * E
    square = 2 * tokens * E * E

    sent = call(
        summarize, shape((sources, HALF + PAD, E), BF16), [SMEM, SMEM, VMEM, VMEM, VMEM, VMEM], "summarize",
        heads * square, 3 * 2 * tokens * heads * E,
    )(first, doc_starts, keys, values, log_decay, gain.reshape(1, E))
    got = lax.all_to_all(sent, PLANE, split_axis=0, concat_axis=0, tiled=True)

    inside, done = [], []
    for s, mine in enumerate(shared(heads)):
        attn, after = call(
                functools.partial(within, heads=mine), (shape((tokens, len(mine) * E), F32), shape((8, E), F32)),
                [SMEM, SMEM, VMEM, VMEM, VMEM, VMEM], f"within{s}", 2 * len(mine) * tri, 5 * 2 * tokens * len(mine) * E,
            )(first, doc_starts, queries, keys, values, log_decay)
        inside.append(attn)
        done.append(after)

    total, gains = call(
        plane_total, (shape((planes, HALF + PAD, E), BF16), shape((heads, E), F32)), [VMEM, ANY], "plane_total",
        4 * sources * HALF * E, 2 * sources * (HALF + PAD) * E,
    )(got, done[0])
    totals = lax.all_to_all(total, "z", split_axis=0, concat_axis=0, tiled=True)
    enter = call(
        entering, shape((sources, HALF, E), BF16), [SMEM, VMEM, VMEM, ANY], "entering",
        4 * sources * HALF * E, 4 * sources * HALF * E,
    )(plane, totals, got, done[1])
    mine = lax.all_to_all(enter, PLANE, split_axis=0, concat_axis=0, tiled=True)
    return call(
        finish, shape((tokens, heads * E), BF16), [SMEM, SMEM] + [VMEM] * (4 + len(inside)), "finish",
        heads * square, 10 * tokens * heads * E,
    )(first, doc_starts, queries, log_decay, *inside, mine, gains)


def solution(mesh):
    ctx, heads = mesh.devices.shape
    split = Mesh(mesh.devices.reshape(ctx // 2, 2, heads // 4, 4), AXES)
    rows = P(AXES, None)
    return jax.shard_map(
        per_device,
        mesh=split,
        in_specs=(rows, rows, rows, rows, P(("y", "x")), P()),
        out_specs=rows,
        check_vma=False,
    )
```

```python
import functools

import jax
import jax.numpy as jnp
from jax import lax
from jax.experimental import pallas as pl
from jax.experimental.pallas import tpu as pltpu
from jax.sharding import Mesh, PartitionSpec as P

E = 128
HALF = E // 2
QUARTER = E // 4
NX = 4
AXES = ("zh", "zl", "core", "y", "x")
NEAR = ("core", "x")
MIDDLE = ("zl", "y")
FAR = "zh"
F32, BF16 = jnp.float32, jnp.bfloat16
SMALL = 14 << 20
VMEM = pl.BlockSpec(memory_space=pltpu.VMEM)
SMEM = pl.BlockSpec(memory_space=pltpu.SMEM)
HBM = pl.BlockSpec(memory_space=pltpu.HBM)


def started(position, starts_ref):
    count = jnp.zeros_like(position)
    for i in range(starts_ref.shape[0] - 1):
        count = count + (position >= starts_ref[i]).astype(jnp.int32)
    return count


def cumulative(decay_ref):
    tokens = decay_ref.shape[1]
    i = lax.broadcasted_iota(jnp.int32, (tokens, tokens), 0)
    j = lax.broadcasted_iota(jnp.int32, (tokens, tokens), 1)
    lower = (i >= j).astype(BF16)
    return lax.dot_general(lower, decay_ref[...], (((1,), (1,)), ((), ())), preferred_element_type=F32)


def parts(value):
    high = value.astype(BF16).astype(F32)
    return high, (value - high).astype(BF16).astype(F32)


def rows_of(values, count):
    row = lax.broadcasted_iota(jnp.int32, (count, E), 0)
    tile = jnp.zeros((count, E), F32)
    for n, value in enumerate(values):
        for i, part in enumerate(parts(value)):
            tile = jnp.where(row == 2 * n + i, jnp.broadcast_to(part, (count, E)), tile)
    return tile.astype(BF16)


def value_of(tile, n):
    return tile[2 * n : 2 * n + 1] + tile[2 * n + 1 : 2 * n + 2]


def column(h):
    return slice(h * E, (h + 1) * E)


def summarize(first_ref, starts_ref, k_ref, v_ref, decay_ref, out_ref, piece_ref, sems):
    heads, tokens = decay_ref.shape
    each = heads // NX
    first = first_ref[0]
    position = first + lax.broadcasted_iota(jnp.int32, (tokens, 1), 0)
    at_end = started(first + tokens - 1, starts_ref)
    cum = cumulative(decay_ref)
    last = cum[tokens - 1 :, :]
    tail = jnp.where(started(position, starts_ref) == at_end, jnp.exp(last - cum), 0.0)
    open_all = at_end == started(first - 1, starts_ref)
    keep = jnp.where(open_all, jnp.exp(last), 0.0)
    copies = []
    for x in range(NX):
        mine = [n * NX + x for n in range(each)]
        for n, h in enumerate(mine):
            scaled = (k_ref[:, column(h)].astype(F32) * tail[:, h : h + 1]).astype(BF16)
            state = lax.dot_general(
                scaled, v_ref[:, column(h)], (((0,), (0,)), ((), ())), preferred_element_type=F32
            ).astype(BF16)
            for c in range(2):
                piece_ref[c * NX + x, n * HALF : (n + 1) * HALF, :] = state[c * HALF : (c + 1) * HALF]
        extra = rows_of([keep[:, h : h + 1] for h in mine], 2 * each)
        for c in range(2):
            p = c * NX + x
            piece_ref[p, each * HALF :, :] = extra
            copies.append(pltpu.make_async_copy(piece_ref.at[p], out_ref.at[p], sems.at[p]))
            copies[-1].start()
    for copy in copies:
        copy.wait()


def within(first_ref, starts_ref, q_ref, k_ref, v_ref, decay_ref, out_ref, done_ref, *, heads):
    done_ref[...] = jnp.zeros_like(done_ref)
    tokens = decay_ref.shape[1]
    first = first_ref[0]
    i = lax.broadcasted_iota(jnp.int32, (tokens, tokens), 0)
    j = lax.broadcasted_iota(jnp.int32, (tokens, tokens), 1)
    mask = (i >= j) & (started(first + i, starts_ref) == started(first + j, starts_ref))
    cum = cumulative(decay_ref)
    across = cum.T
    for n, h in enumerate(heads):
        scores = lax.dot_general(
            q_ref[:, column(n)], k_ref[:, column(n)], (((1,), (1,)), ((), ())), preferred_element_type=F32
        )
        decay = jnp.exp(jnp.where(mask, cum[:, h : h + 1] - across[h : h + 1, :], -1e30))
        weights = (scores * decay).astype(BF16)
        out_ref[:, column(n)] = jnp.dot(weights, v_ref[:, column(n)], preferred_element_type=F32)


def row_total(near_ref, _, out_ref):
    sources, rows = near_ref.shape[0], near_ref.shape[1]
    each = rows // (HALF + 2)
    keeps = [near_ref[p, each * HALF :, :].astype(F32) for p in range(sources)]
    for n in range(each):
        totals = []
        for c in range(2):
            state = near_ref[c * NX, n * HALF : (n + 1) * HALF, :].astype(F32)
            total = value_of(keeps[c * NX], n)
            for x in range(1, NX):
                mine = value_of(keeps[c * NX + x], n)
                state = mine * state + near_ref[c * NX + x, n * HALF : (n + 1) * HALF, :].astype(F32)
                total = mine * total
            for z in range(2):
                out_ref[z * each + n, c * QUARTER : (c + 1) * QUARTER, :] = state[
                    z * QUARTER : (z + 1) * QUARTER
                ].astype(BF16)
            totals.append(total)
        extra = rows_of(totals, 8)
        for z in range(2):
            out_ref[z * each + n, HALF:, :] = extra


def in_order(sources):
    each = sources // 2
    return [(z * each + y, c) for z in range(2) for c in range(2) for y in range(each)]


def block_total(middle_ref, out_ref):
    state, total = jnp.zeros((QUARTER, E), F32), jnp.ones((1, E), F32)
    for p, c in in_order(middle_ref.shape[0]):
        mine = value_of(middle_ref[p, HALF:, :].astype(F32), c)
        state = mine * state + middle_ref[p, c * QUARTER : (c + 1) * QUARTER, :].astype(F32)
        total = mine * total
    state, extra = state.astype(BF16), rows_of([total], 8)
    for z in range(out_ref.shape[0]):
        out_ref[z, 0:QUARTER, :] = state
        out_ref[z, QUARTER:, :] = extra


def enter_rows(block_ref, far_ref, middle_ref, gain_ref, out_ref):
    def earlier(n, state):
        keep = value_of(far_ref[n, QUARTER:, :].astype(F32), 0)
        return keep * state + far_ref[n, 0:QUARTER, :].astype(F32)

    state = lax.fori_loop(0, block_ref[0], earlier, jnp.zeros((QUARTER, E), F32))
    for p, c in in_order(middle_ref.shape[0]):
        out_ref[p, c * QUARTER : (c + 1) * QUARTER, :] = state.astype(BF16)
        mine = value_of(middle_ref[p, HALF:, :].astype(F32), c)
        state = mine * state + middle_ref[p, c * QUARTER : (c + 1) * QUARTER, :].astype(F32)
    extra = rows_of([gain_ref[...]], 8)
    for p in range(out_ref.shape[0]):
        out_ref[p, HALF:, :] = extra


def enter_chunks(middle_ref, near_ref, out_ref, piece_ref, state_ref, sems):
    sources, rows = near_ref.shape[0], near_ref.shape[1]
    each = rows // (HALF + 2)
    gains = [middle_ref[n, HALF:, :] for n in range(each)]
    copies = []
    for c in range(2):
        for x in range(NX):
            p = c * NX + x
            keeps = near_ref[p, each * HALF :, :].astype(F32)
            for n in range(each):
                if x == 0:
                    state = jnp.concatenate(
                        [
                            middle_ref[z * each + n, c * QUARTER : (c + 1) * QUARTER, :].astype(F32)
                            for z in range(2)
                        ]
                    )
                else:
                    state = state_ref[n]
                piece_ref[p, n * HALF : (n + 1) * HALF, :] = state.astype(BF16)
                piece_ref[p, each * HALF + 2 * n : each * HALF + 2 * n + 2, :] = gains[n][0:2]
                if x < NX - 1:
                    state_ref[n] = value_of(keeps, n) * state + near_ref[
                        p, n * HALF : (n + 1) * HALF, :
                    ].astype(F32)
            copies.append(pltpu.make_async_copy(piece_ref.at[p], out_ref.at[p], sems.at[p]))
            copies[-1].start()
    for copy in copies:
        copy.wait()


def finish(first_ref, starts_ref, q_ref, decay_ref, *refs):
    early_ref, late_hbm, enter_ref, out_ref, late_ref, sem = refs
    late = pltpu.make_async_copy(late_hbm, late_ref, sem)
    late.start()
    heads, tokens = decay_ref.shape
    each = heads // NX
    first = first_ref[0]
    position = first + lax.broadcasted_iota(jnp.int32, (tokens, 1), 0)
    opened = started(position, starts_ref) == started(first - 1, starts_ref)
    reach = jnp.where(opened, jnp.exp(cumulative(decay_ref)), 0.0)
    places = [(ref, n) for ref in (early_ref, late_ref) for n in range(ref.shape[1] // E)]
    gains = [enter_ref[x, each * HALF :, :].astype(F32) for x in range(NX)]
    for h in range(heads):
        ref, m = places[h]
        if ref is late_ref and m == 0:
            late.wait()
        n, x = divmod(h, NX)
        state = jnp.concatenate([enter_ref[c * NX + x, n * HALF : (n + 1) * HALF, :] for c in range(2)], axis=0)
        inter = jnp.dot(q_ref[:, column(h)], state, preferred_element_type=F32)
        attn = ref[:, column(m)] + inter * reach[:, h : h + 1]
        meansq = jnp.mean(attn * attn, axis=-1, keepdims=True)
        normed = attn * lax.rsqrt(meansq + 1e-05) * value_of(gains[x], n)
        out_ref[:, column(h)] = normed.astype(BF16)


def call(kernel, out, specs, name, flops, nbytes, limit=None, out_specs=None, scratch=(), grid=()):
    return pl.pallas_call(
        kernel,
        out_shape=out,
        grid=grid,
        in_specs=specs,
        out_specs=jax.tree.map(lambda _: VMEM, out) if out_specs is None else out_specs,
        scratch_shapes=scratch,
        name=name,
        compiler_params=pltpu.CompilerParams(vmem_limit_bytes=limit),
        cost_estimate=pl.CostEstimate(flops=flops, bytes_accessed=nbytes, transcendentals=0),
    )


def exchange(value, axes):
    return lax.all_to_all(value, axes, split_axis=0, concat_axis=0, tiled=True)


def per_device(queries, keys, values, log_decay, gain, doc_starts):
    tokens, heads = log_decay.shape
    each = heads // NX
    far = lax.axis_size(FAR)
    first = (lax.axis_index(AXES) * tokens).astype(jnp.int32).reshape(1)
    block = lax.axis_index(FAR).astype(jnp.int32).reshape(1)
    decay = log_decay.T
    shape = jax.ShapeDtypeStruct
    tri = 2 * tokens * tokens * E
    square = 2 * tokens * E * E
    near_shape = (2 * NX, each * (HALF + 2), E)
    middle_shape = (2 * each, HALF + 8, E)
    near_scratch = pltpu.VMEM(near_shape, BF16)
    near_bytes = 2 * 2 * heads * HALF * E

    sent = call(
        summarize, shape(near_shape, BF16), [SMEM, SMEM, VMEM, VMEM, VMEM], "summarize",
        heads * square, 4 * tokens * heads * E + near_bytes, out_specs=HBM,
        scratch=[near_scratch, pltpu.SemaphoreType.DMA((2 * NX,))],
    )(first, doc_starts, keys, values, decay)
    near = exchange(sent, NEAR)

    inside, done = [], []
    share = heads // 2
    for s in range(2):
        mine = tuple(range(s * share, (s + 1) * share))
        part = pl.BlockSpec((tokens, share * E), functools.partial(lambda s, i: (0, s), s))
        attn, after = call(
            functools.partial(within, heads=mine), (shape((tokens, share * E), F32), shape((8, E), F32)),
            [SMEM, SMEM, part, part, part, pl.BlockSpec((heads, tokens), lambda i: (0, 0))], f"within{s}",
            2 * share * tri, 10 * tokens * share * E, grid=(1,),
            out_specs=(pl.BlockSpec((tokens, share * E), lambda i: (0, 0)), pl.BlockSpec((8, E), lambda i: (0, 0))),
        )(first, doc_starts, queries, keys, values, decay)
        inside.append(attn)
        done.append(after)

    rows = call(
        row_total, shape(middle_shape, BF16), [VMEM, HBM], "row_total", 2 * near_bytes, near_bytes, SMALL,
    )(near, done[0])
    middle = exchange(rows, MIDDLE)
    total = call(
        block_total, shape((far, QUARTER + 8, E), BF16), [VMEM], "block_total", near_bytes, near_bytes // 4, SMALL,
    )(middle)
    totals = exchange(total, FAR)
    row_states = call(
        enter_rows, shape(middle_shape, BF16), [SMEM, VMEM, VMEM, VMEM], "enter_rows", near_bytes, near_bytes // 2, SMALL,
    )(block, totals, middle, gain.reshape(1, E))
    row_states = exchange(row_states, MIDDLE)
    states = call(
        enter_chunks, shape(near_shape, BF16), [VMEM, VMEM], "enter_chunks", 2 * near_bytes, 2 * near_bytes, SMALL,
        out_specs=HBM,
        scratch=[near_scratch, pltpu.VMEM((each, HALF, E), F32), pltpu.SemaphoreType.DMA((2 * NX,))],
    )(row_states, near)
    states = exchange(states, NEAR)
    return call(
        finish, shape((tokens, heads * E), BF16), [SMEM, SMEM, VMEM, VMEM, VMEM, HBM, VMEM], "finish",
        heads * square, 10 * tokens * heads * E, SMALL,
        scratch=[pltpu.VMEM((tokens, share * E), F32), pltpu.SemaphoreType.DMA],
    )(first, doc_starts, queries, decay, *inside, states)


def solution(mesh):
    ctx, heads = mesh.devices.shape
    split = Mesh(mesh.devices.reshape(ctx // 4, 2, 2, heads // NX, NX), AXES)
    rows = P(AXES, None)
    return jax.shard_map(
        per_device,
        mesh=split,
        in_specs=(rows, rows, rows, rows, P(("y", "x")), P()),
        out_specs=rows,
        check_vma=False,
    )
```

```python
import jax
import jax.numpy as jnp
from jax import lax
from jax.experimental import pallas as pl
from jax.experimental.pallas import tpu as pltpu
from jax.sharding import Mesh, PartitionSpec as P

E = 128
HALF = E // 2
QUARTER = E // 4
NS = 8
AXES = ("zh", "zl", "core", "yh", "yl", "x")
NEAR = ("core", "yl", "x")
MIDDLE = ("zl", "yh")
FAR = "zh"
F32, BF16 = jnp.float32, jnp.bfloat16
SMALL = 14 << 20
VMEM = pl.BlockSpec(memory_space=pltpu.VMEM)
SMEM = pl.BlockSpec(memory_space=pltpu.SMEM)
HBM = pl.BlockSpec(memory_space=pltpu.HBM)


def started(position, starts_ref):
    count = jnp.zeros_like(position)
    for i in range(starts_ref.shape[0] - 1):
        count = count + (position >= starts_ref[i]).astype(jnp.int32)
    return count


def cumulative(decay_ref):
    tokens = decay_ref.shape[1]
    i = lax.broadcasted_iota(jnp.int32, (tokens, tokens), 0)
    j = lax.broadcasted_iota(jnp.int32, (tokens, tokens), 1)
    lower = (i >= j).astype(BF16)
    return lax.dot_general(lower, decay_ref[...], (((1,), (1,)), ((), ())), preferred_element_type=F32)


def parts(value):
    high = value.astype(BF16).astype(F32)
    return high, (value - high).astype(BF16).astype(F32)


def rows_of(values, count):
    row = lax.broadcasted_iota(jnp.int32, (count, E), 0)
    tile = jnp.zeros((count, E), F32)
    for n, value in enumerate(values):
        for i, part in enumerate(parts(value)):
            tile = jnp.where(row == 2 * n + i, jnp.broadcast_to(part, (count, E)), tile)
    return tile.astype(BF16)


def value_of(tile, n):
    return tile[2 * n : 2 * n + 1] + tile[2 * n + 1 : 2 * n + 2]


def column(h):
    return slice(h * E, (h + 1) * E)


def summarize(first_ref, starts_ref, k_hbm, v_hbm, decay_ref, out_ref, k_ref, v_ref, piece_ref, in_sems, out_sems):
    heads, tokens = decay_ref.shape
    each = heads // NS
    loads = []
    for n in range(each):
        wide = slice(n * NS * E, (n + 1) * NS * E)
        for i, (source, target) in enumerate(((k_hbm, k_ref), (v_hbm, v_ref))):
            loads.append(pltpu.make_async_copy(source.at[:, wide], target.at[:, wide], in_sems.at[2 * n + i]))
            loads[-1].start()
    first = first_ref[0]
    position = first + lax.broadcasted_iota(jnp.int32, (tokens, 1), 0)
    at_end = started(first + tokens - 1, starts_ref)
    cum = cumulative(decay_ref)
    last = cum[tokens - 1 :, :]
    tail = jnp.where(started(position, starts_ref) == at_end, jnp.exp(last - cum), 0.0)
    open_all = at_end == started(first - 1, starts_ref)
    keep = jnp.where(open_all, jnp.exp(last), 0.0)
    for s in range(NS):
        extra = rows_of([keep[:, n * NS + s : n * NS + s + 1] for n in range(each)], 2 * each)
        for c in range(2):
            piece_ref[c * NS + s, each * HALF :, :] = extra
    copies = []
    for n in range(each):
        loads[2 * n].wait()
        loads[2 * n + 1].wait()
        for s in range(NS):
            h = n * NS + s
            scaled = (k_ref[:, column(h)].astype(F32) * tail[:, h : h + 1]).astype(BF16)
            state = lax.dot_general(
                scaled, v_ref[:, column(h)], (((0,), (0,)), ((), ())), preferred_element_type=F32
            ).astype(BF16)
            for c in range(2):
                piece_ref[c * NS + s, n * HALF : (n + 1) * HALF, :] = state[c * HALF : (c + 1) * HALF]
        end = each * (HALF + 2) if n == each - 1 else (n + 1) * HALF
        block = slice(n * HALF, end)
        copies.append(pltpu.make_async_copy(piece_ref.at[:, block, :], out_ref.at[:, block, :], out_sems.at[n]))
        copies[-1].start()
    for copy in copies:
        copy.wait()


def within(first_ref, starts_ref, q_ref, k_ref, v_ref, decay_ref, out_ref, done_ref):
    done_ref[...] = jnp.zeros_like(done_ref)
    heads, tokens = decay_ref.shape
    first = first_ref[0]
    i = lax.broadcasted_iota(jnp.int32, (tokens, tokens), 0)
    j = lax.broadcasted_iota(jnp.int32, (tokens, tokens), 1)
    mask = (i >= j) & (started(first + i, starts_ref) == started(first + j, starts_ref))
    cum = cumulative(decay_ref)
    across = cum.T
    for h in range(heads):
        scores = lax.dot_general(
            q_ref[:, column(h)], k_ref[:, column(h)], (((1,), (1,)), ((), ())), preferred_element_type=F32
        )
        decay = jnp.exp(jnp.where(mask, cum[:, h : h + 1] - across[h : h + 1, :], -1e30))
        weights = (scores * decay).astype(BF16)
        out_ref[:, column(h)] = jnp.dot(weights, v_ref[:, column(h)], preferred_element_type=F32)


def row_total(near_ref, out_ref):
    sources, rows = near_ref.shape[0], near_ref.shape[1]
    each = rows // (HALF + 2)
    keeps = [near_ref[p, each * HALF :, :].astype(F32) for p in range(sources)]
    for n in range(each):
        totals = []
        for c in range(2):
            state = near_ref[c * NS, n * HALF : (n + 1) * HALF, :].astype(F32)
            total = value_of(keeps[c * NS], n)
            for x in range(1, NS):
                mine = value_of(keeps[c * NS + x], n)
                state = mine * state + near_ref[c * NS + x, n * HALF : (n + 1) * HALF, :].astype(F32)
                total = mine * total
            for z in range(2):
                out_ref[z * each + n, c * QUARTER : (c + 1) * QUARTER, :] = state[
                    z * QUARTER : (z + 1) * QUARTER
                ].astype(BF16)
            totals.append(total)
        extra = rows_of(totals, 8)
        for z in range(2):
            out_ref[z * each + n, HALF:, :] = extra


def in_order(sources):
    each = sources // 2
    return [(z * each + y, c) for z in range(2) for c in range(2) for y in range(each)]


def block_total(middle_ref, out_ref):
    state, total = jnp.zeros((QUARTER, E), F32), jnp.ones((1, E), F32)
    for p, c in in_order(middle_ref.shape[0]):
        mine = value_of(middle_ref[p, HALF:, :].astype(F32), c)
        state = mine * state + middle_ref[p, c * QUARTER : (c + 1) * QUARTER, :].astype(F32)
        total = mine * total
    state, extra = state.astype(BF16), rows_of([total], 8)
    for z in range(out_ref.shape[0]):
        out_ref[z, 0:QUARTER, :] = state
        out_ref[z, QUARTER:, :] = extra


def enter_rows(block_ref, far_ref, middle_ref, gain_ref, _, out_ref):
    def earlier(n, state):
        keep = value_of(far_ref[n, QUARTER:, :].astype(F32), 0)
        return keep * state + far_ref[n, 0:QUARTER, :].astype(F32)

    state = lax.fori_loop(0, block_ref[0], earlier, jnp.zeros((QUARTER, E), F32))
    for p, c in in_order(middle_ref.shape[0]):
        out_ref[p, c * QUARTER : (c + 1) * QUARTER, :] = state.astype(BF16)
        mine = value_of(middle_ref[p, HALF:, :].astype(F32), c)
        state = mine * state + middle_ref[p, c * QUARTER : (c + 1) * QUARTER, :].astype(F32)
    extra = rows_of([gain_ref[...]], 8)
    for p in range(out_ref.shape[0]):
        out_ref[p, HALF:, :] = extra


def enter_chunks(middle_ref, near_ref, out_ref, piece_ref, state_ref, sems):
    sources, rows = near_ref.shape[0], near_ref.shape[1]
    each = rows // (HALF + 2)
    gains = [middle_ref[n, HALF:, :] for n in range(each)]
    copies = []
    for c in range(2):
        for x in range(NS):
            p = c * NS + x
            keeps = near_ref[p, each * HALF :, :].astype(F32)
            for n in range(each):
                if x == 0:
                    state = jnp.concatenate(
                        [
                            middle_ref[z * each + n, c * QUARTER : (c + 1) * QUARTER, :].astype(F32)
                            for z in range(2)
                        ]
                    )
                else:
                    state = state_ref[n]
                piece_ref[p, n * HALF : (n + 1) * HALF, :] = state.astype(BF16)
                piece_ref[p, each * HALF + 2 * n : each * HALF + 2 * n + 2, :] = gains[n][0:2]
                if x < NS - 1:
                    state_ref[n] = value_of(keeps, n) * state + near_ref[
                        p, n * HALF : (n + 1) * HALF, :
                    ].astype(F32)
            copies.append(pltpu.make_async_copy(piece_ref.at[p], out_ref.at[p], sems.at[p]))
            copies[-1].start()
    for copy in copies:
        copy.wait()


def finish(first_ref, starts_ref, q_ref, decay_ref, within_ref, enter_ref, out_hbm, out_ref, sems):
    heads, tokens = decay_ref.shape
    each = heads // NS
    first = first_ref[0]
    position = first + lax.broadcasted_iota(jnp.int32, (tokens, 1), 0)
    opened = started(position, starts_ref) == started(first - 1, starts_ref)
    reach = jnp.where(opened, jnp.exp(cumulative(decay_ref)), 0.0)
    gains = [enter_ref[x, each * HALF :, :].astype(F32) for x in range(NS)]
    copies = []
    for h in range(heads):
        n, x = divmod(h, NS)
        state = jnp.concatenate([enter_ref[c * NS + x, n * HALF : (n + 1) * HALF, :] for c in range(2)], axis=0)
        inter = jnp.dot(q_ref[:, column(h)], state, preferred_element_type=F32)
        attn = within_ref[:, column(h)] + inter * reach[:, h : h + 1]
        meansq = jnp.mean(attn * attn, axis=-1, keepdims=True)
        normed = attn * lax.rsqrt(meansq + 1e-05) * value_of(gains[x], n)
        out_ref[:, column(h)] = normed.astype(BF16)
        if x == NS - 1:
            wide = slice(n * NS * E, (n + 1) * NS * E)
            copies.append(pltpu.make_async_copy(out_ref.at[:, wide], out_hbm.at[:, wide], sems.at[n]))
            copies[-1].start()
    for copy in copies:
        copy.wait()


def call(kernel, out, specs, name, flops, nbytes, limit=None, out_specs=None, scratch=()):
    return pl.pallas_call(
        kernel,
        out_shape=out,
        in_specs=specs,
        out_specs=jax.tree.map(lambda _: VMEM, out) if out_specs is None else out_specs,
        scratch_shapes=scratch,
        name=name,
        compiler_params=pltpu.CompilerParams(vmem_limit_bytes=limit),
        cost_estimate=pl.CostEstimate(flops=flops, bytes_accessed=nbytes, transcendentals=0),
    )


def exchange(value, axes):
    return lax.all_to_all(value, axes, split_axis=0, concat_axis=0, tiled=True)


def per_device(queries, keys, values, log_decay, gain, doc_starts):
    tokens, heads = log_decay.shape
    each = heads // NS
    far = lax.axis_size(FAR)
    first = (lax.axis_index(AXES) * tokens).astype(jnp.int32).reshape(1)
    block = lax.axis_index(FAR).astype(jnp.int32).reshape(1)
    decay = log_decay.T
    shape = jax.ShapeDtypeStruct
    tri = 2 * tokens * tokens * E
    square = 2 * tokens * E * E
    near_shape = (2 * NS, each * (HALF + 2), E)
    middle_shape = (2 * each, HALF + 8, E)
    near_scratch = pltpu.VMEM(near_shape, BF16)
    near_bytes = 2 * 2 * heads * HALF * E

    sent = call(
        summarize, shape(near_shape, BF16), [SMEM, SMEM, HBM, HBM, VMEM], "summarize",
        heads * square, 4 * tokens * heads * E + near_bytes, out_specs=HBM,
        scratch=[
            pltpu.VMEM((tokens, heads * E), BF16), pltpu.VMEM((tokens, heads * E), BF16), near_scratch,
            pltpu.SemaphoreType.DMA((2 * each,)), pltpu.SemaphoreType.DMA((each,)),
        ],
    )(first, doc_starts, keys, values, decay)
    near = exchange(sent, NEAR)

    inside, done = call(
        within, (shape((tokens, heads * E), F32), shape((8, E), F32)),
        [SMEM, SMEM, VMEM, VMEM, VMEM, VMEM], "within", 2 * heads * tri, 10 * tokens * heads * E,
    )(first, doc_starts, queries, keys, values, decay)
    near, done = lax.optimization_barrier((near, done))

    rows = call(
        row_total, shape(middle_shape, BF16), [VMEM], "row_total", 2 * near_bytes, near_bytes, SMALL,
    )(near)
    middle = exchange(rows, MIDDLE)
    total = call(
        block_total, shape((far, QUARTER + 8, E), BF16), [VMEM], "block_total", near_bytes, near_bytes // 4, SMALL,
    )(middle)
    totals = exchange(total, FAR)
    row_states = call(
        enter_rows, shape(middle_shape, BF16), [SMEM, VMEM, VMEM, VMEM, HBM], "enter_rows", near_bytes, near_bytes // 2, SMALL,
    )(block, totals, middle, gain.reshape(1, E), done)
    row_states = exchange(row_states, MIDDLE)
    states = call(
        enter_chunks, shape(near_shape, BF16), [VMEM, VMEM], "enter_chunks", 2 * near_bytes, 2 * near_bytes, SMALL,
        out_specs=HBM,
        scratch=[near_scratch, pltpu.VMEM((each, HALF, E), F32), pltpu.SemaphoreType.DMA((2 * NS,))],
    )(row_states, near)
    states = exchange(states, NEAR)
    return call(
        finish, shape((tokens, heads * E), BF16), [SMEM, SMEM] + [VMEM] * 4, "finish",
        heads * square, 10 * tokens * heads * E, SMALL, out_specs=HBM,
        scratch=[pltpu.VMEM((tokens, heads * E), BF16), pltpu.SemaphoreType.DMA((each,))],
    )(first, doc_starts, queries, decay, inside, states)


def solution(mesh):
    ctx, heads = mesh.devices.shape
    split = Mesh(mesh.devices.reshape(ctx // 4, 2, 2, heads // NS, 2, NS // 2), AXES)
    rows = P(AXES, None)
    return jax.shard_map(
        per_device,
        mesh=split,
        in_specs=(rows, rows, rows, rows, P(("yh", "yl", "x")), P()),
        out_specs=rows,
        check_vma=False,
    )
```

```python
import jax
import jax.numpy as jnp
from jax import lax
from jax.experimental import pallas as pl
from jax.experimental.pallas import tpu as pltpu
from jax.sharding import Mesh, PartitionSpec as P

E = 128
QUARTER = E // 4
PAD = 8
NS = 8
AXES = ("zh", "zl", "core", "yh", "yl", "x")
NEAR = ("yl", "x")
MIDDLE = ("zl", "core", "yh")
FAR = "zh"
F32, BF16 = jnp.float32, jnp.bfloat16
SMALL = 14 << 20
VMEM = pl.BlockSpec(memory_space=pltpu.VMEM)
SMEM = pl.BlockSpec(memory_space=pltpu.SMEM)
HBM = pl.BlockSpec(memory_space=pltpu.HBM)


def started(position, starts_ref):
    count = jnp.zeros_like(position)
    for i in range(starts_ref.shape[0] - 1):
        count = count + (position >= starts_ref[i]).astype(jnp.int32)
    return count


def triangle(tokens, upper):
    i = lax.broadcasted_iota(jnp.int32, (tokens, tokens), 0)
    j = lax.broadcasted_iota(jnp.int32, (tokens, tokens), 1)
    return (i <= j if upper else i >= j).astype(BF16)


def cumulative(decay_ref):
    lower = triangle(decay_ref.shape[1], False)
    return lax.dot_general(lower, decay_ref[...], (((1,), (1,)), ((), ())), preferred_element_type=F32)


def parts(value):
    high = value.astype(BF16).astype(F32)
    return high, (value - high).astype(BF16).astype(F32)


def tile_of(values):
    row = lax.broadcasted_iota(jnp.int32, (PAD, E), 0)
    tile = jnp.zeros((PAD, E), F32)
    for n, value in enumerate(values):
        for i, part in enumerate(parts(value)):
            tile = jnp.where(row == 2 * n + i, jnp.broadcast_to(part, (PAD, E)), tile)
    return tile.astype(BF16)


def value_of(tile, n):
    return tile[2 * n : 2 * n + 1] + tile[2 * n + 1 : 2 * n + 2]


def column(h):
    return slice(h * E, (h + 1) * E)


def summarize(first_ref, starts_ref, k_ref, v_ref, decay_ref, out_ref, piece_ref, sems):
    heads, tokens = decay_ref.shape
    each = heads // NS
    first = first_ref[0]
    position = first + lax.broadcasted_iota(jnp.int32, (1, tokens), 1)
    at_end = started(first + tokens - 1, starts_ref)
    cum = jnp.dot(decay_ref[...], triangle(tokens, True), preferred_element_type=F32)
    last = cum[:, tokens - 1 :]
    tail = jnp.where(started(position, starts_ref) == at_end, jnp.exp(last - cum), 0.0)
    open_all = at_end == started(first - 1, starts_ref)
    keep = jnp.broadcast_to(jnp.where(open_all, jnp.exp(last), 0.0), (heads, E))
    copies = []
    for s in range(NS):
        for n in range(each):
            h = n * NS + s
            scaled = (k_ref[:, column(h)].T.astype(F32) * tail[h : h + 1, :]).astype(BF16)
            state = jnp.dot(scaled, v_ref[:, column(h)], preferred_element_type=F32)
            piece_ref[s, n * E : (n + 1) * E, :] = state.astype(BF16)
        piece_ref[s, each * E :, :] = tile_of([keep[n * NS + s : n * NS + s + 1] for n in range(each)])
        copies.append(pltpu.make_async_copy(piece_ref.at[s], out_ref.at[s], sems.at[s]))
        copies[-1].start()
    for copy in copies:
        copy.wait()


def within(first_ref, starts_ref, q_ref, k_ref, v_ref, decay_ref, out_ref, done_ref):
    done_ref[...] = jnp.zeros_like(done_ref)
    heads, tokens = decay_ref.shape
    first = first_ref[0]
    i = lax.broadcasted_iota(jnp.int32, (tokens, tokens), 0)
    j = lax.broadcasted_iota(jnp.int32, (tokens, tokens), 1)
    mask = (i >= j) & (started(first + i, starts_ref) == started(first + j, starts_ref))
    cum = cumulative(decay_ref)
    across = cum.T
    for h in range(heads):
        scores = lax.dot_general(
            q_ref[:, column(h)], k_ref[:, column(h)], (((1,), (1,)), ((), ())), preferred_element_type=F32
        )
        decay = jnp.exp(jnp.where(mask, cum[:, h : h + 1] - across[h : h + 1, :], -1e30))
        weights = (scores * decay).astype(BF16)
        out_ref[:, column(h)] = jnp.dot(weights, v_ref[:, column(h)], preferred_element_type=F32)


def row_total(near_ref, out_ref):
    each = near_ref.shape[1] // E
    quarters = E // QUARTER
    keeps = [near_ref[s, each * E :, :].astype(F32) for s in range(NS)]
    for n in range(each):
        state, total = near_ref[0, n * E : (n + 1) * E, :].astype(F32), value_of(keeps[0], n)
        for s in range(1, NS):
            mine = value_of(keeps[s], n)
            state = mine * state + near_ref[s, n * E : (n + 1) * E, :].astype(F32)
            total = mine * total
        extra = tile_of([total])
        for r in range(quarters):
            out_ref[r * each + n, 0:QUARTER, :] = state[r * QUARTER : (r + 1) * QUARTER].astype(BF16)
            out_ref[r * each + n, QUARTER:, :] = extra


def after(ref, n, state):
    keep = value_of(ref[n, QUARTER:, :].astype(F32), 0)
    return keep * state + ref[n, 0:QUARTER, :].astype(F32), keep


def block_total(middle_ref, out_ref):
    state, total = jnp.zeros((QUARTER, E), F32), jnp.ones((1, E), F32)
    for n in range(middle_ref.shape[0]):
        state, keep = after(middle_ref, n, state)
        total = keep * total
    state, extra = state.astype(BF16), tile_of([total])
    for z in range(out_ref.shape[0]):
        out_ref[z, 0:QUARTER, :] = state
        out_ref[z, QUARTER:, :] = extra


def enter_rows(block_ref, far_ref, middle_ref, gain_ref, _, out_ref):
    state = lax.fori_loop(
        0, block_ref[0], lambda n, state: after(far_ref, n, state)[0], jnp.zeros((QUARTER, E), F32)
    )
    extra = tile_of([gain_ref[...]])
    for n in range(middle_ref.shape[0]):
        out_ref[n, 0:QUARTER, :] = state.astype(BF16)
        out_ref[n, QUARTER:, :] = extra
        state, _ = after(middle_ref, n, state)


def enter_chunks(middle_ref, near_ref, out_ref):
    each = near_ref.shape[1] // E
    quarters = E // QUARTER
    keeps = [near_ref[s, each * E :, :].astype(F32) for s in range(NS)]
    for n in range(each):
        state = jnp.concatenate([middle_ref[r * each + n, 0:QUARTER, :].astype(F32) for r in range(quarters)])
        for s in range(NS):
            out_ref[s, n * E : (n + 1) * E, :] = state.astype(BF16)
            if s < NS - 1:
                state = value_of(keeps[s], n) * state + near_ref[s, n * E : (n + 1) * E, :].astype(F32)
    row = lax.broadcasted_iota(jnp.int32, (PAD, E), 0)
    gains = jnp.zeros((PAD, E), F32)
    for n in range(each):
        tile = middle_ref[n, QUARTER:, :].astype(F32)
        for i in range(2):
            gains = jnp.where(row == 2 * n + i, jnp.broadcast_to(tile[i : i + 1], (PAD, E)), gains)
    for s in range(NS):
        out_ref[s, each * E :, :] = gains.astype(BF16)


def finish(first_ref, starts_ref, q_ref, decay_ref, within_ref, enter_ref, out_hbm, out_ref, sems):
    heads, tokens = decay_ref.shape
    each = heads // NS
    first = first_ref[0]
    position = first + lax.broadcasted_iota(jnp.int32, (tokens, 1), 0)
    opened = started(position, starts_ref) == started(first - 1, starts_ref)
    reach = jnp.where(opened, jnp.exp(cumulative(decay_ref)), 0.0)
    gains = [enter_ref[s, each * E :, :].astype(F32) for s in range(NS)]
    average = jnp.full((E, E), 1.0 / E, BF16)
    copies = []
    for h in range(heads):
        n, s = divmod(h, NS)
        inter = jnp.dot(q_ref[:, column(h)], enter_ref[s, n * E : (n + 1) * E, :], preferred_element_type=F32)
        attn = within_ref[:, column(h)] + inter * reach[:, h : h + 1]
        meansq = jnp.dot((attn * attn).astype(BF16), average, preferred_element_type=F32)
        normed = attn * lax.rsqrt(meansq + 1e-05) * value_of(gains[s], n)
        out_ref[:, column(h)] = normed.astype(BF16)
        if s == NS - 1:
            wide = slice(n * NS * E, (n + 1) * NS * E)
            copies.append(pltpu.make_async_copy(out_ref.at[:, wide], out_hbm.at[:, wide], sems.at[n]))
            copies[-1].start()
    for copy in copies:
        copy.wait()


def call(kernel, out, specs, name, flops, nbytes, limit=None, out_specs=None, scratch=()):
    return pl.pallas_call(
        kernel,
        out_shape=out,
        in_specs=specs,
        out_specs=jax.tree.map(lambda _: VMEM, out) if out_specs is None else out_specs,
        scratch_shapes=scratch,
        name=name,
        compiler_params=pltpu.CompilerParams(vmem_limit_bytes=limit),
        cost_estimate=pl.CostEstimate(flops=flops, bytes_accessed=nbytes, transcendentals=0),
    )


def exchange(value, axes):
    return lax.all_to_all(value, axes, split_axis=0, concat_axis=0, tiled=True)


def per_device(queries, keys, values, log_decay, gain, doc_starts):
    tokens, heads = log_decay.shape
    each = heads // NS
    far = lax.axis_size(FAR)
    first = (lax.axis_index(AXES) * tokens).astype(jnp.int32).reshape(1)
    block = lax.axis_index(FAR).astype(jnp.int32).reshape(1)
    decay = log_decay.T
    shape = jax.ShapeDtypeStruct
    tri = 2 * tokens * tokens * E
    square = 2 * tokens * E * E
    near_shape = (NS, each * E + PAD, E)
    middle_shape = (4 * each, QUARTER + PAD, E)
    near_bytes = 2 * heads * E * E

    sent = call(
        summarize, shape(near_shape, BF16), [SMEM, SMEM, VMEM, VMEM, VMEM], "summarize",
        heads * square, 4 * tokens * heads * E + near_bytes, out_specs=HBM,
        scratch=[pltpu.VMEM(near_shape, BF16), pltpu.SemaphoreType.DMA((NS,))],
    )(first, doc_starts, keys, values, decay)
    near = exchange(sent, NEAR)

    inside, done = call(
        within, (shape((tokens, heads * E), F32), shape((8, E), F32)),
        [SMEM, SMEM, VMEM, VMEM, VMEM, VMEM], "within", 2 * heads * tri, 10 * tokens * heads * E,
    )(first, doc_starts, queries, keys, values, decay)
    near, done = lax.optimization_barrier((near, done))

    rows = call(
        row_total, shape(middle_shape, BF16), [VMEM], "row_total", 2 * near_bytes, near_bytes, SMALL,
    )(near)
    middle = exchange(rows, MIDDLE)
    total = call(
        block_total, shape((far, QUARTER + PAD, E), BF16), [VMEM], "block_total", near_bytes, near_bytes // 4, SMALL,
    )(middle)
    totals = exchange(total, FAR)
    row_states = call(
        enter_rows, shape(middle_shape, BF16), [SMEM, VMEM, VMEM, VMEM, HBM], "enter_rows", near_bytes, near_bytes // 2, SMALL,
    )(block, totals, middle, gain.reshape(1, E), done)
    row_states = exchange(row_states, MIDDLE)
    states = call(
        enter_chunks, shape(near_shape, BF16), [VMEM, VMEM], "enter_chunks", 2 * near_bytes, 2 * near_bytes, SMALL,
    )(row_states, near)
    states = exchange(states, NEAR)
    return call(
        finish, shape((tokens, heads * E), BF16), [SMEM, SMEM] + [VMEM] * 4, "finish",
        heads * square, 10 * tokens * heads * E, SMALL, out_specs=HBM,
        scratch=[pltpu.VMEM((tokens, heads * E), BF16), pltpu.SemaphoreType.DMA((each,))],
    )(first, doc_starts, queries, decay, inside, states)


def solution(mesh):
    ctx, heads = mesh.devices.shape
    split = Mesh(mesh.devices.reshape(ctx // 4, 2, 2, heads // NS, 2, NS // 2), AXES)
    rows = P(AXES, None)
    return jax.shard_map(
        per_device,
        mesh=split,
        in_specs=(rows, rows, rows, rows, P(("yh", "yl", "x")), P()),
        out_specs=rows,
        check_vma=False,
    )
```

```python
import jax
import jax.numpy as jnp
from jax import lax
from jax.experimental import pallas as pl
from jax.experimental.pallas import tpu as pltpu
from jax.sharding import Mesh, PartitionSpec as P

E = 128
QUARTER = E // 4
PAD = 8
NS = 8
BLOCK_ROWS = 2 * E + PAD
AXES = ("zh", "zl", "core", "yh", "yl", "x")
NEAR = ("yl", "x")
MIDDLE = ("zl", "core", "yh")
FAR = "zh"
F32, BF16 = jnp.float32, jnp.bfloat16
SMALL = 14 << 20
VMEM = pl.BlockSpec(memory_space=pltpu.VMEM)
SMEM = pl.BlockSpec(memory_space=pltpu.SMEM)
HBM = pl.BlockSpec(memory_space=pltpu.HBM)


def started(position, starts_ref):
    count = jnp.zeros_like(position)
    for i in range(starts_ref.shape[0] - 1):
        count = count + (position >= starts_ref[i]).astype(jnp.int32)
    return count


def triangle(tokens, upper):
    i = lax.broadcasted_iota(jnp.int32, (tokens, tokens), 0)
    j = lax.broadcasted_iota(jnp.int32, (tokens, tokens), 1)
    return (i <= j if upper else i >= j).astype(BF16)


def cumulative(decay_ref):
    lower = triangle(decay_ref.shape[1], False)
    return lax.dot_general(lower, decay_ref[...], (((1,), (1,)), ((), ())), preferred_element_type=F32)


def parts(value):
    high = value.astype(BF16).astype(F32)
    middle = (value - high).astype(BF16).astype(F32)
    return high, middle, (value - high - middle).astype(BF16).astype(F32)


def tile_of(values, count=3):
    row = lax.broadcasted_iota(jnp.int32, (PAD, E), 0)
    tile = jnp.zeros((PAD, E), F32)
    for n, value in enumerate(values):
        for i, part in enumerate(parts(value)[:count]):
            tile = jnp.where(row == count * n + i, jnp.broadcast_to(part, (PAD, E)), tile)
    return tile.astype(BF16)


def value_of(tile, n, count=3):
    value = tile[count * n : count * n + 1]
    for i in range(1, count):
        value = value + tile[count * n + i : count * n + i + 1]
    return value


def rows_at(n):
    start = (n // 2) * BLOCK_ROWS + (n % 2) * E
    return slice(start, start + E)


def keep_in(near_ref, s, n):
    start = (n // 2) * BLOCK_ROWS + 2 * E
    return value_of(near_ref[s, start : start + PAD, :].astype(F32), n % 2)


def column(h):
    return slice(h * E, (h + 1) * E)


def summarize(first_ref, starts_ref, k_ref, v_ref, decay_ref, out_ref):
    heads, tokens = decay_ref.shape
    first = first_ref[0]
    position = first + lax.broadcasted_iota(jnp.int32, (1, tokens), 1)
    at_end = started(first + tokens - 1, starts_ref)
    cum = jnp.dot(decay_ref[...], triangle(tokens, True), preferred_element_type=F32)
    last = cum[:, tokens - 1 :]
    tail = jnp.where(started(position, starts_ref) == at_end, jnp.exp(last - cum), 0.0)
    open_all = at_end == started(first - 1, starts_ref)
    keep = jnp.broadcast_to(jnp.where(open_all, jnp.exp(last), 0.0), (heads, E))
    for s in range(NS):
        for n in range(2):
            h = n * NS + s
            scaled = (k_ref[:, column(h)].T.astype(F32) * tail[h : h + 1, :]).astype(BF16)
            state = jnp.dot(scaled, v_ref[:, column(h)], preferred_element_type=F32)
            out_ref[s, n * E : (n + 1) * E, :] = state.astype(BF16)
        out_ref[s, 2 * E :, :] = tile_of([keep[n * NS + s : n * NS + s + 1] for n in range(2)])


def within(first_ref, starts_ref, q_ref, k_ref, v_ref, decay_ref, out_ref, done_ref):
    done_ref[...] = jnp.zeros_like(done_ref)
    heads, tokens = decay_ref.shape
    first = first_ref[0]
    i = lax.broadcasted_iota(jnp.int32, (tokens, tokens), 0)
    j = lax.broadcasted_iota(jnp.int32, (tokens, tokens), 1)
    mask = (i >= j) & (started(first + i, starts_ref) == started(first + j, starts_ref))
    cum = cumulative(decay_ref)
    across = cum.T
    for h in range(heads):
        scores = lax.dot_general(
            q_ref[:, column(h)], k_ref[:, column(h)], (((1,), (1,)), ((), ())), preferred_element_type=F32
        )
        decay = jnp.exp(jnp.where(mask, cum[:, h : h + 1] - across[h : h + 1, :], -1e30))
        weights = (scores * decay).astype(BF16)
        out_ref[:, column(h)] = jnp.dot(weights, v_ref[:, column(h)], preferred_element_type=F32)


def row_total(near_ref, out_ref):
    quarters = E // QUARTER
    each = out_ref.shape[0] // quarters
    for n in range(each):
        state, total = near_ref[0, rows_at(n), :].astype(F32), keep_in(near_ref, 0, n)
        for s in range(1, NS):
            mine = keep_in(near_ref, s, n)
            state = mine * state + near_ref[s, rows_at(n), :].astype(F32)
            total = mine * total
        extra = tile_of([total])
        for r in range(quarters):
            out_ref[r * each + n, 0:QUARTER, :] = state[r * QUARTER : (r + 1) * QUARTER].astype(BF16)
            out_ref[r * each + n, QUARTER:, :] = extra


def after(ref, n, state):
    keep = value_of(ref[n, QUARTER:, :].astype(F32), 0)
    return keep * state + ref[n, 0:QUARTER, :].astype(F32), keep


def block_total(middle_ref, out_ref):
    state, total = jnp.zeros((QUARTER, E), F32), jnp.ones((1, E), F32)
    for n in range(middle_ref.shape[0]):
        state, keep = after(middle_ref, n, state)
        total = keep * total
    state, extra = state.astype(BF16), tile_of([total])
    for z in range(out_ref.shape[0]):
        out_ref[z, 0:QUARTER, :] = state
        out_ref[z, QUARTER:, :] = extra


def enter_rows(block_ref, far_ref, middle_ref, gain_ref, _, out_ref):
    state = lax.fori_loop(
        0, block_ref[0], lambda n, state: after(far_ref, n, state)[0], jnp.zeros((QUARTER, E), F32)
    )
    extra = tile_of([gain_ref[...]], 2)
    for n in range(middle_ref.shape[0]):
        out_ref[n, 0:QUARTER, :] = state.astype(BF16)
        out_ref[n, QUARTER:, :] = extra
        state, _ = after(middle_ref, n, state)


def enter_chunks(middle_ref, near_ref, out_ref):
    quarters = E // QUARTER
    each = middle_ref.shape[0] // quarters
    for n in range(each):
        state = jnp.concatenate([middle_ref[r * each + n, 0:QUARTER, :].astype(F32) for r in range(quarters)])
        for s in range(NS):
            out_ref[s, n * E : (n + 1) * E, :] = state.astype(BF16)
            if s < NS - 1:
                state = keep_in(near_ref, s, n) * state + near_ref[s, rows_at(n), :].astype(F32)
    row = lax.broadcasted_iota(jnp.int32, (PAD, E), 0)
    gains = jnp.zeros((PAD, E), F32)
    for n in range(each):
        tile = middle_ref[n, QUARTER:, :].astype(F32)
        for i in range(2):
            gains = jnp.where(row == 2 * n + i, jnp.broadcast_to(tile[i : i + 1], (PAD, E)), gains)
    for s in range(NS):
        out_ref[s, each * E :, :] = gains.astype(BF16)


def finish(first_ref, starts_ref, q_ref, decay_ref, within_ref, enter_ref, out_hbm, out_ref, sems):
    heads, tokens = decay_ref.shape
    each = heads // NS
    first = first_ref[0]
    position = first + lax.broadcasted_iota(jnp.int32, (tokens, 1), 0)
    opened = started(position, starts_ref) == started(first - 1, starts_ref)
    reach = jnp.where(opened, jnp.exp(cumulative(decay_ref)), 0.0)
    gains = [enter_ref[s, each * E :, :].astype(F32) for s in range(NS)]
    average = jnp.full((E, E), 1.0 / E, BF16)
    copies = []
    for h in range(heads):
        n, s = divmod(h, NS)
        inter = jnp.dot(q_ref[:, column(h)], enter_ref[s, n * E : (n + 1) * E, :], preferred_element_type=F32)
        attn = within_ref[:, column(h)] + inter * reach[:, h : h + 1]
        meansq = jnp.dot((attn * attn).astype(BF16), average, preferred_element_type=F32)
        normed = attn * lax.rsqrt(meansq + 1e-05) * value_of(gains[s], n, 2)
        out_ref[:, column(h)] = normed.astype(BF16)
        if s == NS - 1:
            wide = slice(n * NS * E, (n + 1) * NS * E)
            copies.append(pltpu.make_async_copy(out_ref.at[:, wide], out_hbm.at[:, wide], sems.at[n]))
            copies[-1].start()
    for copy in copies:
        copy.wait()


def call(kernel, out, specs, name, flops, nbytes, limit=None, out_specs=None, scratch=(), grid=()):
    return pl.pallas_call(
        kernel,
        out_shape=out,
        grid=grid,
        in_specs=specs,
        out_specs=jax.tree.map(lambda _: VMEM, out) if out_specs is None else out_specs,
        scratch_shapes=scratch,
        name=name,
        compiler_params=pltpu.CompilerParams(vmem_limit_bytes=limit),
        cost_estimate=pl.CostEstimate(flops=flops, bytes_accessed=nbytes, transcendentals=0),
    )


def exchange(value, axes):
    return lax.all_to_all(value, axes, split_axis=0, concat_axis=0, tiled=True)


def per_device(queries, keys, values, log_decay, gain, doc_starts):
    tokens, heads = log_decay.shape
    each = heads // NS
    far = lax.axis_size(FAR)
    first = (lax.axis_index(AXES) * tokens).astype(jnp.int32).reshape(1)
    block = lax.axis_index(FAR).astype(jnp.int32).reshape(1)
    decay = log_decay.T
    shape = jax.ShapeDtypeStruct
    tri = 2 * tokens * tokens * E
    square = 2 * tokens * E * E
    up_shape = (NS, each // 2 * BLOCK_ROWS, E)
    down_shape = (NS, each * E + PAD, E)
    middle_shape = (4 * each, QUARTER + PAD, E)
    near_bytes = 2 * heads * E * E
    some = pl.BlockSpec((tokens, 2 * NS * E), lambda i: (0, i))

    sent = call(
        summarize, shape(up_shape, BF16),
        [SMEM, SMEM, some, some, pl.BlockSpec((2 * NS, tokens), lambda i: (i, 0))], "summarize",
        heads * square, 4 * tokens * heads * E + near_bytes, grid=(each // 2,),
        out_specs=pl.BlockSpec((NS, BLOCK_ROWS, E), lambda i: (0, i, 0)),
    )(first, doc_starts, keys, values, decay)
    near = exchange(sent, NEAR)

    inside, done = call(
        within, (shape((tokens, heads * E), F32), shape((8, E), F32)),
        [SMEM, SMEM, VMEM, VMEM, VMEM, VMEM], "within", 2 * heads * tri, 10 * tokens * heads * E,
    )(first, doc_starts, queries, keys, values, decay)
    near, done = lax.optimization_barrier((near, done))

    rows = call(
        row_total, shape(middle_shape, BF16), [VMEM], "row_total", 2 * near_bytes, near_bytes, SMALL,
    )(near)
    middle = exchange(rows, MIDDLE)
    total = call(
        block_total, shape((far, QUARTER + PAD, E), BF16), [VMEM], "block_total", near_bytes, near_bytes // 4, SMALL,
    )(middle)
    totals = exchange(total, FAR)
    row_states = call(
        enter_rows, shape(middle_shape, BF16), [SMEM, VMEM, VMEM, VMEM, HBM], "enter_rows", near_bytes, near_bytes // 2, SMALL,
    )(block, totals, middle, gain.reshape(1, E), done)
    row_states = exchange(row_states, MIDDLE)
    states = call(
        enter_chunks, shape(down_shape, BF16), [VMEM, VMEM], "enter_chunks", 2 * near_bytes, 2 * near_bytes, SMALL,
    )(row_states, near)
    states = exchange(states, NEAR)
    return call(
        finish, shape((tokens, heads * E), BF16), [SMEM, SMEM] + [VMEM] * 4, "finish",
        heads * square, 10 * tokens * heads * E, SMALL, out_specs=HBM,
        scratch=[pltpu.VMEM((tokens, heads * E), BF16), pltpu.SemaphoreType.DMA((each,))],
    )(first, doc_starts, queries, decay, inside, states)


def solution(mesh):
    ctx, heads = mesh.devices.shape
    split = Mesh(mesh.devices.reshape(ctx // 4, 2, 2, heads // NS, 2, NS // 2), AXES)
    rows = P(AXES, None)
    return jax.shard_map(
        per_device,
        mesh=split,
        in_specs=(rows, rows, rows, rows, P(("yh", "yl", "x")), P()),
        out_specs=rows,
        check_vma=False,
    )
```
